32 devices in a mesh: wide: 8 (over z, x), narrow: 4 (over y, core).
Axes of the slice: x: 2, y: 2, z: 4, core: 2. Of those that a mesh axis runs over, the one named last changes fastest.
Arguments:
- patches: bfloat16 [128, 256, 768], P(('wide', 'narrow')), may hold values from -6 to 6
- key_lengths: int32 [128], P(('wide', 'narrow')), may hold values from 32 to 256, as said below
- tile_counts: int32 [64], replicated, may hold values from 1 to 4, 128 in all
- ln1_gain: bfloat16 [768], P('narrow'), may hold values from 0.099609375 to 1.8984375
- ln1_bias: bfloat16 [768], P('narrow'), may hold values from -3 to 3
- qkv_weight: bfloat16 [768, 2304], P('narrow'), may hold values from -0.21875 to 0.21875
- query_bias: bfloat16 [768], P('narrow'), may hold values from -3 to 3
- value_bias: bfloat16 [768], P('narrow'), may hold values from -3 to 3
- out_weight: bfloat16 [768, 768], P('narrow'), may hold values from -1.75 to 1.75
- out_bias: bfloat16 [768], P('narrow'), may hold values from -3 to 3
- ln2_gain: bfloat16 [768], P('narrow'), may hold values from 0.099609375 to 1.8984375
- ln2_bias: bfloat16 [768], P('narrow'), may hold values from -3 to 3
- fc1_weight: bfloat16 [768, 3072], P('narrow'), may hold values from -0.21875 to 0.21875
- fc1_bias: bfloat16 [3072], P('narrow'), may hold values from -3 to 3
- fc2_weight: bfloat16 [3072, 768], P('narrow'), may hold values from -0.109375 to 0.109375
- fc2_bias: bfloat16 [768], P('narrow'), may hold values from -3 to 3
- out_cot: bfloat16 [128, 256, 768], P(('wide', 'narrow')), may hold values from -6 to 6
Outputs:
- block_out: bfloat16 [128, 256, 768], P(('wide', 'narrow'))
- patches_grad: float32 [128, 256, 768], P(('wide', 'narrow'))
- ln1_gain_grad: float32 [768], P('narrow')
- ln1_bias_grad: float32 [768], P('narrow')
- qkv_weight_grad: float32 [768, 2304], P('narrow')
- query_bias_grad: float32 [768], P('narrow')
- value_bias_grad: float32 [768], P('narrow')
- out_weight_grad: float32 [768, 768], P('narrow')
- out_bias_grad: float32 [768], P('narrow')
- ln2_gain_grad: float32 [768], P('narrow')
- ln2_bias_grad: float32 [768], P('narrow')
- fc1_weight_grad: float32 [768, 3072], P('narrow')
- fc1_bias_grad: float32 [3072], P('narrow')
- fc2_weight_grad: float32 [3072, 768], P('narrow')
- fc2_bias_grad: float32 [768], P('narrow')
The draws below stay inside these ranges and needn't reach their ends.
Inputs may be any that keep to these rules, and one draw needn't show every extreme that they name: `key_lengths`: sequence 0 has all 256 keys valid; every sequence has at least 32. `tile_counts`: the counts sum to 128; some image has exactly 4.
All inputs are finite; a program needn't handle non-finite values.
Results may differ from the reference program's by a relative error of at most 0.015.
Values may be sent and summed in bfloat16 or wider, within the bound.
A program may use at most 192 MiB of HBM per device.

```python
import math
import jax
import jax.numpy as jnp
import numpy as np
from jax import lax

D = 768
HEADS = 12
HEAD = 64
FF = 3072
L = 256
MIN_KEYS = 32
MOST_TILES = 4
SEQS = 128
IMAGES = 64


def draw_key_lengths(key, part):
    values = jax.random.randint(key, (SEQS,), MIN_KEYS, L + 1)
    return values.at[0].set(L).astype(jnp.int32)


def raised(array, key, source, target, blocks, factor):
    def block_of(dim):
        return (jnp.arange(array.shape[dim]) // (array.shape[dim] // blocks)).reshape((-1,) + (1,) * (array.ndim - 1 - dim))

    near = jax.random.permutation(key, blocks)[block_of(target)]
    second = (block_of(target) + blocks // 2) % blocks
    return jnp.where((block_of(source) == near) | (block_of(source) == second), factor * array, array)


def steps_of(stream_key, shape, split, low, high):
    level, own = 1.0, jax.random.fold_in(stream_key, 6)
    for position, blocks in split:
        draws = jnp.exp(jax.random.uniform(jax.random.fold_in(own, position), (blocks,), jnp.float32, low / len(split), high / len(split)))
        level = level * jnp.repeat(draws, shape[position] // blocks).reshape([-1 if axis == position else 1 for axis in range(len(shape))])
    return level


def split_up(number_of, total, reach, skew):
    portions = [(1 << 20) // math.isqrt(rank ** skew) + 1 for rank in range(2, number_of + 1)]
    spare, counts = total - reach - (number_of - 1), [1] * (number_of - 1)
    while spare > 0:
        movable = [i for i in range(number_of - 1) if counts[i] < reach]
        mass, budget = sum([portions[i] for i in movable]), spare
        for i in movable:
            addition = min(reach - counts[i], max(1, budget * portions[i] // mass), spare)
            counts[i] = counts[i] + addition
            spare = spare - addition
    return np.array([reach] + counts)


def uneven_parts(own_key, amount, total, reach, slope):
    if amount == 2:
        one = jax.random.randint(own_key, (), max(1, total - reach), min(reach, total - 1) + 1)
        return jnp.stack([one, total - one])
    sizes = jnp.asarray(split_up(amount, total, reach, slope), jnp.int32)
    twos = (amount - 1) // 2
    giver, receiver = sizes[1:1 + 2 * twos:2], sizes[2:2 + 2 * twos:2]
    slack = jnp.minimum(giver - 1, reach - receiver)
    shifted = jax.random.randint(jax.random.fold_in(own_key, 1), (twos,), 0, 1 << 20) % (slack + 1)
    sizes = sizes.at[1:1 + 2 * twos:2].set(giver - shifted).at[2:2 + 2 * twos:2].set(receiver + shifted)
    return sizes[jax.random.permutation(jax.random.fold_in(own_key, 2), amount)]


def centred(stream_key, extent, spread, most, shards=(), kind=jnp.bfloat16):
    factor_of = steps_of(stream_key, extent, shards, -0.22, 0.18) if shards else 1.0
    entries = jax.random.normal(stream_key, extent, jnp.float32) * spread * factor_of
    return jnp.minimum(jnp.maximum(entries, -most), most).astype(kind)


def heavy_noise(stream_key, shape, deviation, reach, shards, heavy, kind=jnp.bfloat16):
    values = deviation * jax.random.normal(stream_key, shape, jnp.float32)
    if shards:
        values = values * steps_of(stream_key, shape, shards, -0.22, 0.18)
    return jnp.clip(raised(values, jax.random.fold_in(stream_key, 3), *heavy), -reach, reach).astype(kind)


def setup_inputs(seed: int = 0) -> dict:
    splits = jax.random.split(jax.random.key(seed), 18)
    return {
        "patches": centred(splits[0], (SEQS, L, D), 1.0, 6.0, ((0, 32),)),
        "key_lengths": draw_key_lengths(jax.random.fold_in(splits[17], 71), 0),
        "tile_counts": uneven_parts(splits[2], IMAGES, SEQS, MOST_TILES, 2).astype(jnp.int32),
        "ln1_gain": jnp.clip(1.0 + 0.18 * jax.random.normal(splits[3], (D,), jnp.float32), 0.099609375, 1.8984375).astype(jnp.bfloat16),
        "ln1_bias": centred(splits[4], (D,), 0.5, 3.0, ((0, 4),)),
        "qkv_weight": centred(splits[5], (D, 3 * D), D ** -0.5, 0.21875, ((0, 4),)),
        "query_bias": centred(splits[6], (D,), 0.5, 3.0, ((0, 4),)),
        "value_bias": centred(splits[7], (D,), 0.5, 3.0, ((0, 4),)),
        "out_weight": centred(splits[8], (D, D), (D // 64) ** -0.5, 1.75, ((0, 4),)),
        "out_bias": centred(splits[9], (D,), 0.5, 3.0, ((0, 4),)),
        "ln2_gain": jnp.clip(1.0 + 0.18 * jax.random.normal(splits[10], (D,), jnp.float32), 0.099609375, 1.8984375).astype(jnp.bfloat16),
        "ln2_bias": centred(splits[11], (D,), 0.5, 3.0, ((0, 4),)),
        "fc1_weight": centred(splits[12], (D, FF), D ** -0.5, 0.21875, ((0, 4),)),
        "fc1_bias": centred(splits[13], (FF,), 0.5, 3.0, ((0, 4),)),
        "fc2_weight": centred(splits[14], (FF, D), FF ** -0.5, 0.109375, ((0, 4),)),
        "fc2_bias": centred(splits[15], (D,), 0.5, 3.0, ((0, 4),)),
        "out_cot": heavy_noise(splits[16], (SEQS, L, D), 1.0, 6.0, ((0, 32),), (0, 2, 32, 2.75)),
    }


@jax.custom_vjp
def low(v):
    return lax.optimization_barrier(v.astype(jnp.bfloat16)).astype(jnp.float32)

@jax.custom_vjp
def low_back(v):
    return v

def low_keep(v):
    return (low(v), None)

def low_pass(kept, grad):
    return (grad,)

def back_keep(v):
    return (v, None)

def back_low(kept, grad):
    return (low(grad),)
low.defvjp(low_keep, low_pass)
low_back.defvjp(back_keep, back_low)
eps = 1e-06
masked_score = -1e+30
highest = lax.Precision.HIGHEST

def normalize(rows, gain, shift):
    mean = lax.optimization_barrier(jnp.mean(rows, axis=-1, keepdims=True))
    centered = rows - mean
    variance = lax.optimization_barrier(jnp.mean(centered * centered, axis=-1, keepdims=True))
    return centered * lax.rsqrt(variance + eps) * gain + shift

def attend_pair(item):
    query, keys, values, valid = item
    scale = HEAD ** (-0.5)
    scores = jnp.einsum('sqhe,skhe->shqk', query, keys, precision=highest) * scale
    place = lax.broadcasted_iota(jnp.int32, scores.shape, 3)
    scores = jnp.where(place < valid[:, None, None, None], scores, masked_score)
    scores = low_back(scores)
    probs = low(jax.nn.softmax(scores, axis=-1))
    return jnp.einsum('shqk,skhe->sqhe', probs, values, precision=highest)

def layer(patch_rows, params, valid):
    ln1_gain, ln1_bias, qkv_weight, query_bias, value_bias, out_weight, out_bias, ln2_gain, ln2_bias, fc1_weight, fc1_bias, fc2_weight, fc2_bias = params
    count = patch_rows.shape[0]
    rows = patch_rows.reshape(-1, D)
    h_one = low(normalize(rows, ln1_gain, ln1_bias))
    qkv_bias = jnp.concatenate([query_bias, jnp.zeros_like(query_bias), value_bias])
    qkv = low(low_back(jnp.dot(h_one, qkv_weight, precision=highest) + qkv_bias))
    blocks = qkv.reshape(count // 2, 2, L, 3, HEADS, HEAD)
    attended = lax.map(jax.checkpoint(attend_pair), (blocks[:, :, :, 0], blocks[:, :, :, 1], blocks[:, :, :, 2], valid.reshape(count // 2, 2)))
    attended = low(low_back(attended.reshape(-1, D)))
    middle = rows + low_back(jnp.dot(attended, out_weight, precision=highest)) + out_bias
    h_two = low(normalize(middle, ln2_gain, ln2_bias))
    before = low_back(jnp.dot(h_two, fc1_weight, precision=highest)) + fc1_bias
    active = low(jax.nn.gelu(before, approximate=False))
    return middle + low_back(jnp.dot(active, fc2_weight, precision=highest)) + fc2_bias

def reference(patches, key_lengths, tile_counts, ln1_gain, ln1_bias, qkv_weight, query_bias, value_bias, out_weight, out_bias, ln2_gain, ln2_bias, fc1_weight, fc1_bias, fc2_weight, fc2_bias, out_cot):
    params = tuple((weight.astype(jnp.float32) for weight in (ln1_gain, ln1_bias, qkv_weight, query_bias, value_bias, out_weight, out_bias, ln2_gain, ln2_bias, fc1_weight, fc1_bias, fc2_weight, fc2_bias)))
    ends = jnp.cumsum(tile_counts)
    starts = ends - tile_counts
    seq_ids = jnp.arange(SEQS, dtype=jnp.int32)
    inside = (starts[None, :] <= seq_ids[:, None]) & (seq_ids[:, None] < ends[None, :])
    counts_seq = lax.optimization_barrier(jnp.sum(jnp.where(inside, tile_counts[None, :], 0), axis=1))
    seq_weight = 1.0 / counts_seq.astype(jnp.float32)
    cot = out_cot.astype(jnp.float32) * seq_weight[:, None, None]
    group = math.gcd(SEQS, 16)
    inputs = patches.astype(jnp.float32).reshape(SEQS // group, group, L, D)
    valid_groups = key_lengths.reshape(SEQS // group, group)
    cot_groups = cot.reshape(SEQS // group, group, L, D)

    def step(totals, item):
        block, valid, block_cot = item
        result, pull = jax.vjp(lambda xx, pp: layer(xx, pp, valid), block, params)
        d_block, d_params = pull(block_cot.reshape(-1, D))
        totals = tuple((a + b for a, b in zip(totals, d_params)))
        return (totals, (result.reshape(block.shape), d_block.reshape(block.shape)))
    start = tuple((jnp.zeros_like(weight) for weight in params))
    totals, (results, d_inputs) = lax.scan(step, start, (inputs, valid_groups, cot_groups))
    block_out = results.reshape(SEQS, L, D).astype(jnp.bfloat16)
    patches_grad = d_inputs.reshape(SEQS, L, D)
    return (block_out, patches_grad, totals[0], totals[1], totals[2], totals[3], totals[4], totals[5], totals[6], totals[7], totals[8], totals[9], totals[10], totals[11], totals[12])
```

```python
from functools import partial

import jax
import jax.numpy as jnp
from jax import lax
from jax.experimental import pallas as pl
from jax.experimental.pallas import tpu as pltpu
from jax.sharding import PartitionSpec as P

D = 768
FF = 3072
QW = 2304
L = 256
HP = 6
TOK = 1024
NSEQ = 4
EPS = 1e-6
NEG = -1e30
SCALE = 0.125
CH = 9
NS = 3
MESH = pl.DeviceIdType.MESH
BF = jnp.bfloat16
F32 = jnp.float32


def mm(a, b):
    return lax.dot_general(a, b, (((1,), (0,)), ((), ())), preferred_element_type=F32)


def mm_nt(a, b):
    return lax.dot_general(a, b, (((1,), (1,)), ((), ())), preferred_element_type=F32)


def ds(start, size, mult=None):
    if isinstance(start, int):
        return pl.ds(start, size)
    return pl.ds(pl.multiple_of(start, size if mult is None else mult), size)


def unit_of(x):
    mean = jnp.mean(x, axis=-1, keepdims=True)
    cen = x - mean
    inv = lax.rsqrt(jnp.mean(cen * cen, axis=-1, keepdims=True) + EPS)
    return cen * inv, inv


def norm_back(grad, unit, inv, gain):
    s = grad * gain
    return inv * (
        s - jnp.mean(s, axis=-1, keepdims=True) - unit * jnp.mean(s * unit, axis=-1, keepdims=True)
    )


def gelu_pair(x):
    e = jnp.exp(x * x * -0.5)
    t = 1.0 / (1.0 + jnp.abs(x) * (0.3275911 * 0.7071067811865476))
    poly = 0.5 * 1.061405429
    poly = poly * t + 0.5 * -1.453152027
    poly = poly * t + 0.5 * 1.421413741
    poly = poly * t + 0.5 * -0.284496736
    poly = poly * t + 0.5 * 0.254829592
    tail = poly * t * e
    cdf = jnp.where(x >= 0, 1.0 - tail, tail)
    return x * cdf, cdf + x * e * 0.3989422804014327


def colsum(x):
    return jnp.sum(x, axis=0, keepdims=True)


def kernel(
    extra,
    comm,
    klen,
    counts,
    pvec,
    patches,
    cot,
    wq,
    wo,
    w1,
    w2,
    bo_out,
    pg_out,
    gqo_out,
    g1_out,
    g2_out,
    v_out,
    Wq,
    Wo,
    W1,
    W2,
    QKV,
    N1,
    N2,
    AT,
    HT,
    GT,
    PT,
    CB,
    MID,
    OUT,
    DH,
    ACT,
    DPR,
    LSE,
    PB,
    PV,
    B1,
    SW,
    V,
    VB,
    VR,
    VZ,
    VE,
    G,
    RC,
    RY,
    A,
    RX,
    RZ,
    F,
    RE,
    lsem,
    fsem,
    psem,
    ocs,
    ocr,
    gys,
    gyr,
    gxs,
    gxr,
    g1s,
    g1r,
    g2s,
    g2r,
    cs,
    cr,
    credit,
    ys,
    yr,
    xs,
    xr,
    zs,
    zr,
    es,
    er,
    zgs,
    zgr,
    xgs,
    xgr,
    vs,
    vr,
):
    w = lax.axis_index("wide")
    n = lax.axis_index("narrow")
    c = lax.rem(n, 2)
    yy = lax.div(n, 2)
    nc = n + 1 - 2 * c
    ny = lax.rem(n + 2, 4)
    nd = lax.rem(nc + 2, 4)
    b = lax.rem(w, 2)
    wx = w + 1 - 2 * b
    z = lax.rem(lax.div(w, 2), 4)
    zt = [lax.rem(z + k, 4) for k in range(4)]
    wz = [w + 2 * (zt[k] - z) for k in range(4)]
    zf = [lax.rem(z + 4 - k, 4) for k in range(4)]
    we = [w + (8 << e) * (1 - 2 * lax.rem(lax.div(w, 8 << e), 2)) for e in range(extra)]
    core, ypart, diag, xpart = (w, nc), (w, ny), (w, nd), (wx, n)
    zpart = [(wz[k], n) for k in range(4)]
    epart = [(we[e], n) for e in range(extra)]

    def put(src, dst, ss, rs, dev):
        return pltpu.make_async_remote_copy(
            src_ref=src, dst_ref=dst, send_sem=ss, recv_sem=rs, device_id=dev, device_id_type=MESH
        )

    sent = []

    def send(src, dst, ss, rs, dev):
        if not comm:
            return None
        cp = put(src, dst, ss, rs, dev)
        cp.start()
        sent.append(cp)
        return cp

    def got(dst, ss, rs, dev):
        if comm:
            put(dst, dst, ss, rs, dev).wait_recv()

    def settle(cp):
        if cp is not None:
            cp.wait_send()
            sent[:] = [one for one in sent if one is not cp]

    halfrows = [(Wq, wq, 192, 0), (Wo, wo, 192, 0), (W1, w1, 192, 0)]
    patch_cp = pltpu.make_async_copy(patches, PT, lsem.at[0])
    patch_cp.start()
    cot_cp = pltpu.make_async_copy(cot, CB, lsem.at[1])
    cot_cp.start()
    own = [
        pltpu.make_async_copy(wq, Wq.at[ds(n * 192, 192)], lsem.at[2]),
        pltpu.make_async_copy(wo, Wo.at[ds(n * 192, 192)], lsem.at[3]),
        pltpu.make_async_copy(w1, W1.at[ds(n * 192, 192)], lsem.at[4]),
    ] + [
        pltpu.make_async_copy(
            w2.at[pl.ds(256 * j, 256)], W2.at[j, ds(n * 256, 256)], lsem.at[5 + j]
        )
        for j in range(3)
    ]
    for cp in own:
        cp.start()
    pv_cp = pltpu.make_async_copy(pvec, PB.at[n], lsem.at[8])
    pv_cp.start()

    if comm:
        bar = pltpu.get_barrier_semaphore()
        partners = [core, ypart, diag, xpart] + zpart[1:] + epart
        for dev in partners:
            pl.semaphore_signal(bar, inc=1, device_id=dev, device_id_type=MESH)
        pl.semaphore_wait(bar, len(partners))

    pieces = []
    for i in range(3):
        pieces.append(
            (
                lambda h, i=i: wq.at[ds(h * 96, 96), pl.ds(768 * i, 768)],
                lambda m, h, i=i: Wq.at[ds(m * 192 + h * 96, 96), pl.ds(768 * i, 768)],
            )
        )
    pieces.append(
        (
            lambda h: wo.at[ds(h * 96, 96)],
            lambda m, h: Wo.at[ds(m * 192 + h * 96, 96)],
        )
    )
    for i in range(3):
        pieces.append(
            (
                lambda h, i=i: w1.at[ds(h * 96 + 32 * i, 32)],
                lambda m, h, i=i: W1.at[ds(m * 192 + h * 96 + 32 * i, 32)],
            )
        )
    for j in range(3):
        pieces.append(
            (
                lambda h, j=j: w2.at[ds(256 * j + h * 128, 128)],
                lambda m, h, j=j: W2.at[j, ds(m * 256 + h * 128, 128)],
            )
        )
    ocopies = []
    for i in range(3):
        ocopies.append(
            (
                wq.at[:, pl.ds(768 * i, 768)],
                lambda m, i=i: Wq.at[ds(m * 192, 192), pl.ds(768 * i, 768)],
            )
        )
    ocopies.append((wo, lambda m: Wo.at[ds(m * 192, 192)]))
    ocopies.append((w1, lambda m: W1.at[ds(m * 192, 192)]))
    for j in range(3):
        ocopies.append((w2.at[pl.ds(256 * j, 256)], lambda m, j=j: W2.at[j, ds(m * 256, 256)]))

    def y_start(p):
        send(pieces[p][0](b), pieces[p][1](n, b), gys.at[p], gyr.at[p], ypart)

    def y_pass(p):
        at = pieces[p][1](ny, b)
        got(at, gys.at[p], gyr.at[p], ypart)
        send(at, at, gxs.at[p], gxr.at[p], xpart)
        send(at, at, g1s.at[p], g1r.at[p], core)

    def x_pass(p):
        at = pieces[p][1](ny, 1 - b)
        got(at, gxs.at[p], gxr.at[p], xpart)
        send(at, at, g2s.at[p], g2r.at[p], core)

    def c_wait(p):
        got(pieces[p][1](nd, b), g1s.at[p], g1r.at[p], core)
        got(pieces[p][1](nd, 1 - b), g2s.at[p], g2r.at[p], core)

    def o_wait(q):
        got(ocopies[q][1](nc), ocs.at[q], ocr.at[q], core)

    for k, dev in enumerate((core, ypart, diag)):
        send(pvec, PB.at[n], psem.at[0, k], psem.at[1, k], dev)
    y_start(0)
    y_start(1)
    y_start(2)
    for q in range(len(ocopies)):
        send(ocopies[q][0], ocopies[q][1](n), ocs.at[q], ocr.at[q], core)

    im = counts.shape[1]
    cnt = jnp.broadcast_to(counts[...].astype(F32), (8, im))
    ti = lax.broadcasted_iota(jnp.int32, (im, im), 0)
    tj = lax.broadcasted_iota(jnp.int32, (im, im), 1)
    tri = jnp.where(ti <= tj, 1.0, 0.0).astype(BF)
    ends = mm(cnt.astype(BF), tri)
    starts = ends - cnt
    first = (w * 4 + n) * NSEQ
    for q in range(NSEQ):
        sid = (first + q).astype(F32)
        inside = (starts <= sid) & (sid < ends)
        total = jnp.sum(jnp.where(inside, cnt, 0.0), axis=1, keepdims=True)
        SW[q] = jnp.broadcast_to(1.0 / total, (8, 128))

    cot_cp.wait()
    fc2b = jnp.zeros((1, D), F32)
    for q in range(NSEQ):
        g = CB[pl.ds(q * L, L), :].astype(F32) * SW[q][0:1, 0:1]
        fc2b = fc2b + colsum(g)
        gb = g.astype(BF)
        CB[pl.ds(q * L, L), :] = gb
        GT[:, pl.ds(q * L, L)] = gb.T
    V[...] = jnp.zeros_like(V)
    V[7:8, :] = fc2b

    pv_cp.wait()
    got(PB.at[nc], psem.at[0, 0], psem.at[1, 0], core)
    got(PB.at[ny], psem.at[0, 1], psem.at[1, 1], ypart)
    got(PB.at[nd], psem.at[0, 2], psem.at[1, 2], diag)
    ri = lax.broadcasted_iota(jnp.int32, (256, D), 0)
    rj = lax.broadcasted_iota(jnp.int32, (256, D), 1)
    pv = jnp.zeros((16, D), F32)
    for m in range(4):
        blk = PB[m]
        sel = jnp.where((rj - ri == 192 * m) & (ri < 192), 1.0, 0.0).astype(BF)
        pv = pv + mm(blk, sel)
        wide_blk = blk.astype(F32)
        for i in range(6):
            B1[:, pl.ds(768 * m + 128 * i, 128)] = wide_blk[8 + i : 9 + i, 0:128]
    PV[...] = pv

    patch_cp.wait()
    ln1g, ln1b = PV[0:1, :], PV[1:2, :]

    def ln1_step(r, carry):
        rows = ds(r * L, L)
        unit, _ = unit_of(PT[rows, :].astype(F32))
        N1[rows, :] = (unit * ln1g + ln1b).astype(BF)
        return carry

    lax.fori_loop(0, NSEQ, ln1_step, 0)

    for cp in own:
        cp.wait()
    y_pass(0)
    y_start(3)
    y_pass(1)
    y_start(4)
    for i in range(3):
        if i == 1:
            y_pass(2)
            y_start(5)
        x_pass(i)
        o_wait(i)
        c_wait(i)

        def qkv_step(r, carry, i=i):
            rows = ds(r * L, L)
            t = mm(N1[rows, :], Wq[:, pl.ds(768 * i, 768)])
            if i == 0:
                t = t + PV[2:3, :]
            if i == 2:
                t = t + PV[3:4, :]
            QKV[rows, pl.ds(768 * i, 768)] = t.astype(BF)
            return carry

        lax.fori_loop(0, NSEQ, qkv_step, 0)
    y_pass(3)
    y_start(6)
    lane = lax.broadcasted_iota(jnp.int32, (1, 128), 1)
    low = jnp.where(lane < 64, 1.0, 0.0)
    masks = (low.astype(BF), (1.0 - low).astype(BF))
    lowf = lane < 64
    keypos = lax.broadcasted_iota(jnp.int32, (L, L), 0)

    def attend(seq):
        valid = keypos < klen[seq]

        def step(hp, carry):
            rows = ds(seq * L, L)
            q = QKV[rows, ds(hp * 128, 128)] * BF(SCALE)
            k = QKV[rows, ds(D + hp * 128, 128)]
            v = QKV[rows, ds(2 * D + hp * 128, 128)]
            vt = v.T
            outs = []
            for h in range(2):
                s = jnp.where(valid, mm_nt(k, q * masks[h]), NEG)
                top = jnp.max(s, axis=0, keepdims=True)
                e = jnp.exp(s - top)
                tot = colsum(e)
                LSE[seq * 2 * HP + hp * 2 + h] = top + jnp.log(tot)
                p = (e * (1.0 / tot)).astype(BF)
                outs.append(mm(vt, p)[64 * h : 64 * h + 64, :])
            o = jnp.concatenate(outs, axis=0).astype(BF)
            AT[ds(hp * 128, 128), ds(seq * L, L)] = o
            N1[rows, ds(hp * 128, 128)] = o.T
            return carry

        lax.fori_loop(0, HP, step, 0)

    attend(0)
    x_pass(3)
    y_pass(4)
    y_start(7)
    attend(1)
    x_pass(4)
    y_pass(5)
    y_start(8)
    attend(2)
    x_pass(5)
    y_pass(6)
    y_start(9)
    attend(3)
    x_pass(6)
    o_wait(3)
    c_wait(3)

    def out_step(r, carry):
        rows = ds(r * L, L)
        mid = PT[rows, :].astype(F32) + mm(N1[rows, :], Wo[...]) + PV[4:5, :]
        MID[rows, :] = mid
        OUT[rows, :] = mid + PV[7:8, :]
        unit, _ = unit_of(mid)
        h2 = (unit * PV[5:6, :] + PV[6:7, :]).astype(BF)
        N2[rows, :] = h2
        HT[:, rows] = h2.T
        DH[rows, :] = jnp.zeros((L, D), F32)
        return carry

    lax.fori_loop(0, NSEQ, out_step, 0)
    y_pass(7)
    o_wait(4)
    for p in (4, 5, 6):
        c_wait(p)
    x_pass(7)

    gcopies = {}

    def acquire(i):
        if i >= NS:
            for cp in gcopies.pop(i - NS):
                settle(cp)

    def step0(i):
        slot = i % NS
        if i >= NS and comm:
            pl.semaphore_wait(credit, 1)
        gcopies[i] = [
            send(
                G.at[slot, 2 * t + 1 - c], RC.at[slot, t], cs.at[i, t], cr.at[i, t], core
            )
            for t in range(2)
        ]

    def addto(dst, one, two, rows, strip=64):
        def step(r, carry):
            sl = ds(r * strip, strip)
            dst[sl, :] = (one[sl, :].astype(F32) + two[sl, :].astype(F32)).astype(BF)
            return carry

        lax.fori_loop(0, rows // strip, step, 0)

    def step1(i):
        slot = i % NS
        got(RC.at[slot, 0], cs.at[i, 0], cr.at[i, 0], core)
        got(RC.at[slot, 1], cs.at[i, 1], cr.at[i, 1], core)
        gs = G.at[slot, ny]
        addto(gs, gs, RC.at[slot, 1 - yy], 768)
        gcopies[i].append(send(gs, RY.at[i], ys.at[i], yr.at[i], ypart))
        addto(A.at[i], G.at[slot, n], RC.at[slot, yy], 768)
        if i + NS < CH and comm:
            pl.semaphore_signal(credit, inc=1, device_id=core, device_id_type=MESH)

    def step2(i):
        got(RY.at[i], ys.at[i], yr.at[i], ypart)
        other, mine = ds((1 - b) * 384, 384), ds(b * 384, 384)
        addto(A.at[i, other], A.at[i, other], RY.at[i, other], 384)
        send(A.at[i, other], RX.at[i], xs.at[i], xr.at[i], xpart)
        addto(A.at[i, mine], A.at[i, mine], RY.at[i, mine], 384)

    def step3(i):
        got(RX.at[i], xs.at[i], xr.at[i], xpart)
        mine = ds(b * 384, 384)
        addto(A.at[i, mine], A.at[i, mine], RX.at[i], 384)
        for k in range(1, 4):
            send(
                A.at[i, ds(b * 384 + zt[k] * 96, 96)],
                RZ.at[i, k - 1],
                zs.at[i, k - 1],
                zr.at[i, k - 1],
                zpart[k],
            )

    def place(i, half, part):
        p = half * 4 + part
        cb, rh = lax.div(p, 2), lax.rem(p, 2)
        if i < 6 and i % 2 == 0:
            return g2_out.at[ds(p * 96, 96), pl.ds((i // 2) * 256, 256)]
        if i < 6:
            return g1_out.at[ds(rh * 96, 96), ds(cb * 768 + (i // 2) * 256, 256)]
        if i == 6:
            return gqo_out.at[ds(rh * 96, 96), ds(cb * 256, 256)]
        blk = 4 * (i - 6) + cb - 3
        col = D + lax.rem(blk, 3) * D + lax.div(blk, 3) * 256
        return gqo_out.at[ds(rh * 96, 96), ds(col, 256)]

    locals_ = []

    def step4(i):
        for k in range(1, 4):
            got(RZ.at[i, k - 1], zs.at[i, k - 1], zr.at[i, k - 1], zpart[k])
        t = A[i, ds(b * 384 + z * 96, 96), :].astype(F32)
        for k in range(3):
            t = t + RZ[i, k].astype(F32)
        F[i] = t.astype(BF)
        last = F.at[i]
        for e in range(extra):
            send(last, RE.at[i, 2 * e], es.at[i, e], er.at[i, e], epart[e])
            got(RE.at[i, 2 * e], es.at[i, e], er.at[i, e], epart[e])
            RE[i, 2 * e + 1] = (last[...].astype(F32) + RE[i, 2 * e].astype(F32)).astype(BF)
            last = RE.at[i, 2 * e + 1]
        at = place(i, b, z)
        cp = pltpu.make_async_copy(last, at, fsem.at[i])
        cp.start()
        locals_.append(cp)
        for k in range(1, 4):
            send(last, at, zgs.at[i, k - 1], zgr.at[i, k - 1], zpart[k])
        send(last, at, xgs.at[i, 0], xgr.at[i, 0], xpart)

    def step5(i):
        for k in range(1, 4):
            at = place(i, b, zf[k])
            got(at, zgs.at[i, k - 1], zgr.at[i, k - 1], zpart[k])
            send(at, at, xgs.at[i, k], xgr.at[i, k], xpart)

    def step6(i):
        for k in range(4):
            got(place(i, 1 - b, zf[k]), xgs.at[i, k], xgr.at[i, k], xpart)

    steps = (step0, step1, step2, step3, step4, step5, step6)

    def run(*todo):
        for k, i in todo:
            if 0 <= i < CH:
                steps[k](i)

    for j in range(3):
        if j == 0:
            o_wait(5)
            c_wait(7)
        if j == 1:
            o_wait(6)
            c_wait(8)
        if j == 2:
            o_wait(7)
            c_wait(9)
        acquire(2 * j)
        acquire(2 * j + 1)
        s2, s1 = (2 * j) % NS, (2 * j + 1) % NS
        for u in range(2):

            def hidden(t, carry, j=j, u=u):
                s = 2 * u + t
                col = ds(s * 768 + j * 256, 256)
                tc = ds(t * 256, 256)
                bias = B1[:, col]
                w1s = W1[:, col]
                w2s = W2[j, ds(s * 256, 256), :]
                tot = jnp.zeros((1, 256), F32)
                for r in range(2):
                    rows = pl.ds(r * 512, 512)
                    act, slope = gelu_pair(mm(N2[rows, :], w1s) + bias)
                    ACT[rows, tc] = act.astype(BF)
                    dpre = mm_nt(CB[rows, :], w2s) * slope
                    tot = tot + colsum(dpre)
                    DPR[rows, tc] = dpre.astype(BF)
                V[ds(8 + s, 1, 1), pl.ds(j * 256, 256)] = tot
                G[s2, s] = mm(GT[...], ACT[:, tc]).astype(BF)
                return carry

            lax.fori_loop(0, 2, hidden, 0)
            if u == 1:
                step0(2 * j)

            def wgrad(t, carry, j=j, u=u):
                s = 2 * u + t
                res = mm(HT[...], DPR[:, ds(t * 256, 256)]).astype(BF)
                for m in range(4):
                    G[s1, m, ds(s * 192, 192), :] = res[192 * m : 192 * m + 192, :]
                return carry

            lax.fori_loop(0, 2, wgrad, 0)
            if u == 1:
                step0(2 * j + 1)
                step1(2 * j)
            else:
                if j == 0:
                    y_pass(8)
                    x_pass(8)
                if j == 1:
                    run((2, 0))
                if j == 2:
                    run((2, 2), (3, 0), (3, 1))

            def accum(r, carry, j=j, u=u):
                rows = ds(r * L, L)
                OUT[rows, :] += mm(ACT[rows, :], W2[j, pl.ds(u * 512, 512), :])
                t = jnp.zeros((L, D), F32)
                for q in range(2):
                    t = t + mm_nt(
                        DPR[rows, pl.ds(q * 256, 256)],
                        W1[:, pl.ds((2 * u + q) * 768 + j * 256, 256)],
                    )
                DH[rows, :] += t
                return carry

            lax.fori_loop(0, NSEQ, accum, 0)
            if u == 1:
                step1(2 * j + 1)
                if j == 0:
                    y_pass(9)
                    x_pass(9)
                if j == 1:
                    run((2, 1))
                if j == 2:
                    run((2, 3), (4, 0), (4, 1), (3, 2))

    cot2 = pltpu.make_async_copy(cot, CB, lsem.at[1])
    cot2.start()

    def bo_step(r, carry):
        rows = ds(r * L, L)
        N1[rows, :] = OUT[rows, :].astype(BF)
        return carry

    lax.fori_loop(0, NSEQ, bo_step, 0)
    bo_cp = pltpu.make_async_copy(N1, bo_out, lsem.at[9])
    bo_cp.start()
    cot2.wait()

    def ln2_step(r, carry):
        sg, sb, so = carry
        rows = ds(r * L, L)
        dh = DH[rows, :]
        unit, inv = unit_of(MID[rows, :])
        g2 = CB[rows, :].astype(F32) * SW[r][0:1, 0:1] + norm_back(dh, unit, inv, PV[5:6, :])
        DH[rows, :] = g2
        g2b = g2.astype(BF)
        N2[rows, :] = g2b
        CB[rows, :] = mm_nt(g2b, Wo[...]).astype(BF)
        unit1, _ = unit_of(PT[rows, :].astype(F32))
        GT[:, rows] = (unit1 * PV[0:1, :] + PV[1:2, :]).astype(BF).T
        return sg + colsum(dh * unit), sb + colsum(dh), so + colsum(g2)

    zero = jnp.zeros((1, D), F32)
    sg, sb, so = lax.fori_loop(0, NSEQ, ln2_step, (zero, zero, zero))
    V[4:5, :] = so
    V[5:6, :] = sg
    V[6:7, :] = sb
    run((2, 4), (3, 3), (4, 2), (5, 0), (5, 1))

    def grad_block(blk, left, right):
        slot, cb = (6 + blk // 4) % NS, blk % 4
        res = mm(left[...], right).astype(BF)
        for m in range(4):
            G[slot, m, pl.ds(cb * 192, 192), :] = res[192 * m : 192 * m + 192, :]

    acquire(6)
    for i in range(3):
        grad_block(i, AT, N2[:, pl.ds(256 * i, 256)])

    def attend_back(seq, hq):
        valid = keypos < klen[seq]

        def step(t, carry):
            hp = 2 * hq + t
            rows = ds(seq * L, L)
            cq, ck, cv = ds(hp * 128, 128), ds(D + hp * 128, 128), ds(2 * D + hp * 128, 128)
            q = QKV[rows, cq] * BF(SCALE)
            k = QKV[rows, ck]
            v = QKV[rows, cv]
            do = CB[rows, cq]
            kt = k.T
            dq, dk, dv = [], [], []
            for h in range(2):
                s = jnp.where(valid, mm_nt(k, q * masks[h]), NEG)
                p = jnp.exp(s - LSE[seq * 2 * HP + hp * 2 + h])
                dp = mm_nt(v, do * masks[h])
                dsc = (p * (dp - colsum(dp * p))).astype(BF)
                dv.append(mm(p.astype(BF), do))
                dk.append(mm(dsc, q))
                dq.append(mm(kt, dsc)[64 * h : 64 * h + 64, :])
            dqt = (jnp.concatenate(dq, axis=0) * SCALE).astype(BF)
            QKV[rows, cq] = dqt.T
            QKV[rows, ck] = jnp.where(lowf, dk[0], dk[1]).astype(BF)
            QKV[rows, cv] = jnp.where(lowf, dv[0], dv[1]).astype(BF)
            return carry

        lax.fori_loop(0, 2, step, 0)

    for hq in range(3):

        def seq_step(seq, carry, hq=hq):
            attend_back(seq, hq)
            return carry

        lax.fori_loop(0, NSEQ, seq_step, 0)
        cols = [pl.ds(t * D + hq * 256, 256) for t in range(3)]
        for t in range(3):
            blk = 3 + 3 * hq + t
            if blk % 4 == 0:
                acquire(6 + blk // 4)
            grad_block(blk, GT, QKV[:, cols[t]])
            if blk % 4 == 3:
                step0(6 + blk // 4)
        V[2:3, pl.ds(hq * 256, 256)] = colsum(QKV[:, cols[0]].astype(F32))
        V[3:4, pl.ds(hq * 256, 256)] = colsum(QKV[:, cols[2]].astype(F32))
        if hq == 0:
            run((1, 6), (2, 5), (3, 4), (4, 3), (5, 2))
        if hq == 1:
            run((1, 7), (3, 5), (4, 4), (5, 3), (2, 6))
        if hq == 2:
            run((1, 8), (4, 5), (5, 4), (3, 6))

    def ln1_back(r, carry):
        sg, sb = carry
        rows = ds(r * L, L)
        dh = mm_nt(QKV[rows, :], Wq[...])
        unit, inv = unit_of(PT[rows, :].astype(F32))
        MID[rows, :] = DH[rows, :] + norm_back(dh, unit, inv, PV[0:1, :])
        return sg + colsum(dh * unit), sb + colsum(dh)

    carry = (zero, zero)
    for r in range(2):
        carry = lax.fori_loop(2 * r, 2 * r + 2, ln1_back, carry)
        if r == 0:
            run((2, 7), (5, 5), (4, 6))
    V[0:1, :] = carry[0]
    V[1:2, :] = carry[1]
    pg_cp = pltpu.make_async_copy(MID, pg_out, lsem.at[10])
    pg_cp.start()

    send(V, VR.at[0], vs.at[0], vr.at[0], core)
    run((3, 7), (2, 8), (5, 6))
    got(VR.at[0], vs.at[0], vr.at[0], core)
    VB[0] = V[...] + VR[0]
    send(VB.at[0], VR.at[1], vs.at[1], vr.at[1], ypart)
    run((4, 7))
    got(VR.at[1], vs.at[1], vr.at[1], ypart)
    VB[1] = VB[0] + VR[1]
    send(VB.at[1], VR.at[2], vs.at[2], vr.at[2], xpart)
    run((3, 8))
    got(VR.at[2], vs.at[2], vr.at[2], xpart)
    VB[2] = VB[1] + VR[2]
    VZ[z] = VB[2]
    for k in range(1, 4):
        send(VB.at[2], VZ.at[z], vs.at[2 + k], vr.at[2 + k], zpart[k])
    run((5, 7), (4, 8))
    for k in range(1, 4):
        got(VZ.at[zf[k]], vs.at[2 + k], vr.at[2 + k], zpart[k])
    tot = VZ[0] + VZ[1] + VZ[2] + VZ[3]
    for e in range(extra):
        VE[2 * e] = tot
        send(VE.at[2 * e], VE.at[2 * e + 1], vs.at[6 + e], vr.at[6 + e], epart[e])
        got(VE.at[2 * e + 1], vs.at[6 + e], vr.at[6 + e], epart[e])
        tot = tot + VE[2 * e + 1]
    v_out[...] = tot
    run((5, 8))
    for i in range(CH):
        step6(i)
    for cp in list(sent):
        cp.wait_send()
    for cp in locals_:
        cp.wait()
    bo_cp.wait()
    pg_cp.wait()


def layer_call(extra, args, comm=True):
    any_, vmem, smem = (
        pl.BlockSpec(memory_space=s) for s in (pl.ANY, pltpu.VMEM, pltpu.SMEM)
    )
    dma, reg = pltpu.SemaphoreType.DMA, pltpu.SemaphoreType.REGULAR
    ex = max(extra, 1)
    scratch = [
        pltpu.VMEM((D, QW), BF),
        pltpu.VMEM((D, D), BF),
        pltpu.VMEM((D, FF), BF),
        pltpu.VMEM((3, 1024, D), BF),
        pltpu.VMEM((TOK, QW), BF),
        pltpu.VMEM((TOK, D), BF),
        pltpu.VMEM((TOK, D), BF),
        pltpu.VMEM((D, TOK), BF),
        pltpu.VMEM((D, TOK), BF),
        pltpu.VMEM((D, TOK), BF),
        pltpu.VMEM((TOK, D), BF),
        pltpu.VMEM((TOK, D), BF),
        pltpu.VMEM((TOK, D), F32),
        pltpu.VMEM((TOK, D), F32),
        pltpu.VMEM((TOK, D), F32),
        pltpu.VMEM((TOK, 512), BF),
        pltpu.VMEM((TOK, 512), BF),
        pltpu.VMEM((NSEQ * 2 * HP, 1, L), F32),
        pltpu.VMEM((4, 16, 256), BF),
        pltpu.VMEM((16, D), F32),
        pltpu.VMEM((1, FF), F32),
        pltpu.VMEM((NSEQ, 8, 128), F32),
        pltpu.VMEM((16, D), F32),
        pltpu.VMEM((3, 16, D), F32),
        pltpu.VMEM((3, 16, D), F32),
        pltpu.VMEM((4, 16, D), F32),
        pltpu.VMEM((2 * ex, 16, D), F32),
        pltpu.VMEM((NS, 4, D, 256), BF),
        pltpu.VMEM((NS, 2, D, 256), BF),
        pltpu.VMEM((CH, D, 256), BF),
        pltpu.VMEM((CH, D, 256), BF),
        pltpu.VMEM((CH, 384, 256), BF),
        pltpu.VMEM((CH, 3, 96, 256), BF),
        pltpu.VMEM((CH, 96, 256), BF),
        pltpu.VMEM((CH if extra else 1, 2 * ex, 96 if extra else 16, 256), BF),
        dma((11,)),
        dma((CH,)),
        dma((2, 3)),
        dma((8,)),
        dma((8,)),
    ]
    scratch += [dma((10,))] * 8
    scratch += [dma((CH, 2)), dma((CH, 2)), reg]
    scratch += [dma((CH,))] * 4
    scratch += [dma((CH, 3))] * 2
    scratch += [dma((CH, ex))] * 2
    scratch += [dma((CH, 3))] * 2
    scratch += [dma((CH, 4))] * 2
    scratch += [dma((6 + ex,))] * 2
    out_shape = (
        jax.ShapeDtypeStruct((TOK, D), BF),
        jax.ShapeDtypeStruct((TOK, D), F32),
        jax.ShapeDtypeStruct((192, D + QW), BF),
        jax.ShapeDtypeStruct((192, FF), BF),
        jax.ShapeDtypeStruct((D, D), BF),
        jax.ShapeDtypeStruct((16, D), F32),
    )
    return pl.pallas_call(
        partial(kernel, extra, comm),
        out_shape=out_shape,
        in_specs=[smem, vmem] + [any_] * 7,
        out_specs=[any_] * 5 + [vmem],
        scratch_shapes=scratch,
        compiler_params=pltpu.CompilerParams(
            collective_id=0 if comm else None, has_side_effects=True, vmem_limit_bytes=66 * 1000 * 1000
        ),
        name="layer",
    )(*args)


def body(
    comm,
    extra,
    patches,
    key_lengths,
    tile_counts,
    ln1_gain,
    ln1_bias,
    qkv_weight,
    query_bias,
    value_bias,
    out_weight,
    out_bias,
    ln2_gain,
    ln2_bias,
    fc1_weight,
    fc1_bias,
    fc2_weight,
    fc2_bias,
    out_cot,
):
    vecs = jnp.stack(
        [ln1_gain, ln1_bias, query_bias, value_bias, out_bias, ln2_gain, ln2_bias, fc2_bias]
    )
    pvec = jnp.concatenate(
        [
            jnp.pad(vecs, ((0, 0), (0, 64))),
            jnp.pad(fc1_bias.reshape(6, 128), ((0, 2), (0, 128))),
        ]
    )
    bo, pg, gqo, g1, g2t, vec = layer_call(
        extra,
        (
            key_lengths,
            tile_counts.reshape(1, -1),
            pvec,
            patches.reshape(TOK, D),
            out_cot.reshape(TOK, D),
            qkv_weight,
            out_weight,
            fc1_weight,
            fc2_weight,
        ),
        comm,
    )
    n = lax.axis_index("narrow")
    part = lax.dynamic_slice(vec, (0, n * 192), (8, 192))
    fc1b = lax.dynamic_slice(vec, (8 + n, 0), (1, D))[0]
    return (
        bo.reshape(patches.shape),
        pg.reshape(patches.shape),
        part[0],
        part[1],
        gqo[:, D:].astype(F32),
        part[2],
        part[3],
        gqo[:, :D].astype(F32),
        part[4],
        part[5],
        part[6],
        g1.astype(F32),
        fc1b,
        g2t.T.astype(F32),
        part[7],
    )


def solution(mesh, comm=True):
    extra = (mesh.shape["wide"] // 8).bit_length() - 1
    rows3 = P(("wide", "narrow"), None, None)
    mat, vec = P("narrow", None), P("narrow")
    in_specs = (
        rows3,
        P(("wide", "narrow")),
        P(),
        vec,
        vec,
        mat,
        vec,
        vec,
        mat,
        vec,
        vec,
        vec,
        mat,
        vec,
        mat,
        vec,
        rows3,
    )
    out_specs = (
        rows3,
        rows3,
        vec,
        vec,
        mat,
        vec,
        vec,
        mat,
        vec,
        vec,
        vec,
        mat,
        vec,
        mat,
        vec,
    )
    return jax.shard_map(
        partial(body, comm, extra), mesh=mesh, in_specs=in_specs, out_specs=out_specs, check_vma=False
    )
```

```python
from functools import partial

import jax
import jax.numpy as jnp
from jax import lax
from jax.experimental import pallas as pl
from jax.experimental.pallas import tpu as pltpu
from jax.sharding import PartitionSpec as P

D = 768
FF = 3072
QW = 2304
L = 256
HP = 6
TOK = 1024
NSEQ = 4
EPS = 1e-6
NEG = -1e30
SCALE = 0.125
CH = 9
NC = 10
NP = 16
NS = 3
AU = 2
BU = 2
MESH = pl.DeviceIdType.MESH
BF = jnp.bfloat16
F32 = jnp.float32


def mm(a, b):
    return lax.dot_general(a, b, (((1,), (0,)), ((), ())), preferred_element_type=F32)


def mm_nt(a, b):
    return lax.dot_general(a, b, (((1,), (1,)), ((), ())), preferred_element_type=F32)


def ds(start, size, mult=None):
    if isinstance(start, int):
        return pl.ds(start, size)
    return pl.ds(pl.multiple_of(start, size if mult is None else mult), size)


def unit_of(x):
    mean = jnp.mean(x, axis=-1, keepdims=True)
    cen = x - mean
    inv = lax.rsqrt(jnp.mean(cen * cen, axis=-1, keepdims=True) + EPS)
    return cen * inv, inv


def norm_back(grad, unit, inv, gain):
    s = grad * gain
    return inv * (
        s - jnp.mean(s, axis=-1, keepdims=True) - unit * jnp.mean(s * unit, axis=-1, keepdims=True)
    )


def gelu_pair(x):
    cdf = 0.5 * lax.erf(x * 0.7071067811865476) + 0.5
    return x * cdf, cdf + x * jnp.exp(x * x * -0.5) * 0.3989422804014327


def colsum(x):
    return jnp.sum(x, axis=0, keepdims=True)


def scoped(label, fn):
    def call(i):
        with jax.named_scope(f"{label}_{i}" if isinstance(i, int) else label):
            return fn(i)

    return call


def loop(label, lo, hi, fn, init):
    with jax.named_scope(label):
        return lax.fori_loop(lo, hi, fn, init)


def kernel(
    extra,
    comm,
    klen,
    counts,
    l1g,
    l1b,
    qbias,
    vbias,
    obias,
    l2g,
    l2b,
    f2b,
    f1b,
    patches,
    cot,
    wq,
    wo,
    w1,
    w2,
    bo_out,
    pg_out,
    g_out,
    v_out,
    Wq,
    Wo,
    W1,
    W2,
    QKV,
    N1,
    N2,
    AT,
    HT,
    GT,
    PT,
    CB,
    MID,
    OUT,
    DH,
    ACT,
    DPR,
    LSE,
    PB,
    OWN,
    PV,
    B1,
    QB,
    SW,
    V,
    VB,
    VR,
    VE,
    G,
    RC,
    RY,
    A,
    RX,
    RZ,
    RE,
    lsem,
    fsem,
    psem,
    ocs,
    ocr,
    gys,
    gyr,
    gxs,
    gxr,
    g1s,
    g1r,
    g2s,
    g2r,
    cs,
    cr,
    credit,
    ys,
    yr,
    xs,
    xr,
    zs,
    zr,
    es,
    er,
    zgs,
    zgr,
    xgs,
    xgr,
    vs,
    vr,
):
    w = lax.axis_index("wide")
    n = lax.axis_index("narrow")
    c = lax.rem(n, 2)
    yy = lax.div(n, 2)
    nc = n + 1 - 2 * c
    ny = lax.rem(n + 2, 4)
    nd = lax.rem(nc + 2, 4)
    b = lax.rem(w, 2)
    wx = w + 1 - 2 * b
    z = lax.rem(lax.div(w, 2), 4)
    zt = [lax.rem(z + k, 4) for k in range(4)]
    wz = [w + 2 * (zt[k] - z) for k in range(4)]
    zf = [lax.rem(z + 4 - k, 4) for k in range(4)]
    we = [w + (8 << e) * (1 - 2 * lax.rem(lax.div(w, 8 << e), 2)) for e in range(extra)]
    core, ypart, diag, xpart = (w, nc), (w, ny), (w, nd), (wx, n)
    zpart = [(wz[k], n) for k in range(4)]
    epart = [(we[e], n) for e in range(extra)]

    def put(src, dst, ss, rs, dev):
        return pltpu.make_async_remote_copy(
            src_ref=src, dst_ref=dst, send_sem=ss, recv_sem=rs, device_id=dev, device_id_type=MESH
        )

    sent = []

    def send(src, dst, ss, rs, dev):
        if not comm:
            return None
        cp = put(src, dst, ss, rs, dev)
        cp.start()
        sent.append(cp)
        return cp

    def got(dst, ss, rs, dev):
        if comm:
            put(dst, dst, ss, rs, dev).wait_recv()

    def settle(cp):
        if cp is not None:
            cp.wait_send()
            sent[:] = [one for one in sent if one is not cp]

    halfrows = [(Wq, wq, 192, 0), (Wo, wo, 192, 0), (W1, w1, 192, 0)]
    patch_cp = pltpu.make_async_copy(patches, PT, lsem.at[0])
    patch_cp.start()
    cot_cp = pltpu.make_async_copy(cot, CB, lsem.at[1])
    cot_cp.start()
    own = [
        pltpu.make_async_copy(wq, Wq.at[ds(n * 192, 192)], lsem.at[2]),
        pltpu.make_async_copy(wo, Wo.at[ds(n * 192, 192)], lsem.at[3]),
        pltpu.make_async_copy(w1, W1.at[ds(n * 192, 192)], lsem.at[4]),
    ] + [
        pltpu.make_async_copy(
            w2.at[pl.ds(256 * j, 256)], W2.at[j, ds(n * 256, 256)], lsem.at[5 + j]
        )
        for j in range(3)
    ]
    for cp in own:
        cp.start()
    OWN[...] = jnp.zeros_like(OWN)
    for r, one in enumerate((l1g, l1b, qbias, vbias, obias, l2g, l2b, f2b)):
        OWN[r, 0:192] = one[...].astype(F32)
    OWN[8, :] = f1b[...].astype(F32)
    PB[n] = OWN[...]

    partners = [core, ypart, diag, xpart] + zpart[1:] + epart
    if comm:
        bar = pltpu.get_barrier_semaphore()
        for dev in partners:
            pl.semaphore_signal(bar, inc=1, device_id=dev, device_id_type=MESH)

    NQ = 9
    pieces = [
        (
            lambda h: wo.at[ds(h * 96, 96)],
            lambda m, h: Wo.at[ds(m * 192 + h * 96, 96)],
        )
    ]
    for i in range(3):
        pieces.append(
            (
                lambda h, i=i: w1.at[ds(h * 96 + 32 * i, 32)],
                lambda m, h, i=i: W1.at[ds(m * 192 + h * 96 + 32 * i, 32)],
            )
        )
    for j in range(3):
        pieces.append(
            (
                lambda h, j=j: w2.at[ds(256 * j + h * 128, 128)],
                lambda m, h, j=j: W2.at[j, ds(m * 256 + h * 128, 128)],
            )
        )

    def qcol(p):
        return ds(lax.rem(p, 3) * D + lax.div(p, 3) * 256, 256)

    def source(p, h):
        if isinstance(p, int) and p >= NQ:
            return pieces[p - NQ][0](h)
        return wq.at[ds(h * 96, 96), qcol(p)]

    def spot(p, m, h):
        if isinstance(p, int) and p >= NQ:
            return pieces[p - NQ][1](m, h)
        return Wq.at[ds(m * 192 + h * 96, 96), qcol(p)]

    ocopies = [(wq, lambda m: Wq.at[ds(m * 192, 192)])]
    ocopies.append((wo, lambda m: Wo.at[ds(m * 192, 192)]))
    ocopies.append((w1, lambda m: W1.at[ds(m * 192, 192)]))
    for j in range(3):
        ocopies.append((w2.at[pl.ds(256 * j, 256)], lambda m, j=j: W2.at[j, ds(m * 256, 256)]))

    def y_copy(p, m):
        if isinstance(p, int) and p == 0:
            src, dst = wq.at[:, pl.ds(0, 256)], Wq.at[ds(m * 192, 192), pl.ds(0, 256)]
        else:
            src, dst = source(p, b), spot(p, m, b)
        return src, dst, gys.at[p], gyr.at[p], ypart

    def go(src, dst, ss, rs, dev):
        if comm:
            put(src, dst, ss, rs, dev).start()

    def gone(src, dst, ss, rs, dev):
        if comm:
            put(src, dst, ss, rs, dev).wait_send()

    @partial(scoped, "y_start")
    def y_start(p):
        go(*y_copy(p, n))

    def passes(p):
        mine, other = spot(p, ny, b), spot(p, ny, 1 - b)
        return (
            (mine, mine, gxs.at[p], gxr.at[p], xpart),
            (mine, mine, g1s.at[p], g1r.at[p], core),
            (other, other, g2s.at[p], g2r.at[p], core),
        )

    @partial(scoped, "y_pass")
    def y_pass(p):
        src, dst, *rest = y_copy(p, ny)
        got(dst, *rest)
        over_x, mine, other = passes(p)
        go(*mine)
        if isinstance(p, int) and p == 0:
            go(*other)
        else:
            go(*over_x)

    @partial(scoped, "x_pass")
    def x_pass(p):
        got(spot(p, ny, 1 - b), gxs.at[p], gxr.at[p], xpart)
        go(*passes(p)[2])

    @partial(scoped, "c_wait")
    def c_wait(p):
        got(spot(p, nd, b), g1s.at[p], g1r.at[p], core)
        got(spot(p, nd, 1 - b), g2s.at[p], g2r.at[p], core)

    @partial(scoped, "o_wait")
    def o_wait(q):
        got(ocopies[q][1](nc), ocs.at[q], ocr.at[q], core)

    def gather_done():
        for p in range(NP):
            gone(*y_copy(p, n))
            over_x, mine, other = passes(p)
            gone(*mine)
            gone(*other)
            if p:
                gone(*over_x)

    im = counts.shape[1]
    cnt = jnp.broadcast_to(counts[...].astype(F32), (8, im))
    ti = lax.broadcasted_iota(jnp.int32, (im, im), 0)
    tj = lax.broadcasted_iota(jnp.int32, (im, im), 1)
    tri = jnp.where(ti <= tj, 1.0, 0.0).astype(BF)
    ends = mm(cnt.astype(BF), tri)
    starts = ends - cnt
    first = (w * 4 + n) * NSEQ
    for q in range(NSEQ):
        sid = (first + q).astype(F32)
        inside = (starts <= sid) & (sid < ends)
        total = jnp.sum(jnp.where(inside, cnt, 0.0), axis=1, keepdims=True)
        SW[q] = jnp.broadcast_to(1.0 / total, (8, 128))

    with jax.named_scope('cot_wait'):
        cot_cp.wait()
    fc2b = jnp.zeros((1, D), F32)
    for q in range(NSEQ):
        with jax.named_scope('cotangent'):
            g = CB[pl.ds(q * L, L), :].astype(F32) * SW[q][0:1, 0:1]
            fc2b = fc2b + colsum(g)
            gb = g.astype(BF)
            CB[pl.ds(q * L, L), :] = gb
            GT[:, pl.ds(q * L, L)] = gb.T
    V[...] = jnp.zeros_like(V)
    V[7:8, :] = fc2b

    if comm:
        with jax.named_scope("barrier"):
            pl.semaphore_wait(bar, len(partners))

    for k, dev in enumerate((core, ypart, diag)):
        send(OWN, PB.at[n], psem.at[0, k], psem.at[1, k], dev)
    for p in range(NP):
        y_start(p)
    for q in range(len(ocopies)):
        send(ocopies[q][0], ocopies[q][1](n), ocs.at[q], ocr.at[q], core)

    got(PB.at[nc], psem.at[0, 0], psem.at[1, 0], core)
    got(PB.at[ny], psem.at[0, 1], psem.at[1, 1], ypart)
    got(PB.at[nd], psem.at[0, 2], psem.at[1, 2], diag)
    for m in range(4):
        PV[0:8, 192 * m : 192 * m + 192] = PB[m, 0:8, 0:192]
        B1[:, pl.ds(768 * m, 768)] = PB[m, 8:9, :]
    pv = PV[...]
    QB[:, 0:D] = pv[2:3, :]
    QB[:, D : 2 * D] = jnp.zeros((1, D), F32)
    QB[:, 2 * D : 3 * D] = pv[3:4, :]

    patch_cp.wait()
    ln1g, ln1b = PV[0:1, :], PV[1:2, :]

    def ln1_step(r, carry):
        rows = ds(r * L, L)
        unit, _ = unit_of(PT[rows, :].astype(F32))
        N1[rows, :] = (unit * ln1g + ln1b).astype(BF)
        return carry

    loop('first_norm', 0, NSEQ, ln1_step, 0)

    for cp in own:
        cp.wait()
    for p in range(3):
        y_pass(p)
    o_wait(0)

    def project(hq):
        def qkv_step(t, carry):
            p = 3 * hq + t
            c_wait(p)
            col = qcol(p)
            QKV[:, col] = (mm(N1[...], Wq[:, col]) + QB[:, col]).astype(BF)
            return carry

        loop("qkv", 0, 3, qkv_step, 0)

    lane = lax.broadcasted_iota(jnp.int32, (1, 128), 1)
    low = jnp.where(lane < 64, 1.0, 0.0)
    masks = (low.astype(BF), (1.0 - low).astype(BF))
    spare = (jnp.where(lane == 64, 1.0, 0.0), jnp.where(lane == 0, 1.0, 0.0))
    sparelow = tuple(one.astype(BF) for one in spare)
    lowf = lane < 64
    keypos = lax.broadcasted_iota(jnp.int32, (L, 128), 0)

    def scores(q, k, drop, h):
        return mm_nt(k * masks[h] + drop[h], q * masks[h] + sparelow[h])

    def drops(seq):
        out = jnp.where(keypos < klen[seq], 0.0, NEG)
        return tuple((out * spare[h]).astype(BF) for h in range(2))

    def attend(hq, lo):
        def one(seq, hp, drop):
            rows = ds(seq * L, L)
            q = QKV[rows, ds(hp * 128, 128)] * BF(SCALE)
            k = QKV[rows, ds(D + hp * 128, 128)]
            vt = QKV[rows, ds(2 * D + hp * 128, 128)].T
            outs = []
            for h in range(2):
                s = scores(q, k, drop, h)
                top = jnp.max(s, axis=0, keepdims=True)
                e = jnp.exp(s - top)
                tot = colsum(e)
                LSE[ds(seq * 2 * HP + hp * 2 + h, 1, 1), :] = top + jnp.log(tot)
                outs.append(mm(vt[64 * h : 64 * h + 64, :], e.astype(BF)) * (1.0 / tot))
            o = jnp.concatenate(outs, axis=0).astype(BF)
            AT[ds(hp * 128, 128), ds(seq * L, L)] = o
            N2[rows, ds(hp * 128, 128)] = o.T

        def step(seq, carry):
            drop = drops(seq)
            for t in range(2):
                one(seq, 2 * hq + t, drop)
            return carry

        loop("attend", lo, lo + 2, step, 0)

    between = {
        (0, 0): ((x_pass, 1), (y_pass, 3), (x_pass, 2)),
        (0, 1): ((y_pass, 4), (y_pass, 5), (x_pass, 3)),
        (0, 2): ((x_pass, 4), (x_pass, 5), (y_pass, 6), (y_pass, 7)),
        (0, 3): ((x_pass, 6), (x_pass, 7), (y_pass, 8)),
        (1, 0): (),
        (1, 1): ((x_pass, 8), (y_pass, 9), (y_pass, 10)),
        (1, 2): ((x_pass, 9),),
        (1, 3): ((y_pass, 11),),
        (2, 0): (),
        (2, 1): ((x_pass, 10),),
        (2, 2): ((y_pass, 12),),
        (2, 3): ((x_pass, 11),),
    }

    def serve(*key):
        for fn, i in between[key]:
            fn(i)

    for hq in range(3):
        serve(hq, 0)
        project(hq)
        serve(hq, 1)
        attend(hq, 0)
        serve(hq, 2)
        attend(hq, 2)
        serve(hq, 3)
    o_wait(1)
    c_wait(9)

    def out_block(i, carry):
        col = ds(i * 256, 256)
        MID[:, col] = PT[:, col].astype(F32) + mm(N2[...], Wo[:, col]) + PV[4:5, col]
        return carry

    loop("out_proj", 0, 3, out_block, 0)
    y_pass(13)
    x_pass(12)

    def out_step(r, carry):
        rows = ds(r * L, L)
        mid = MID[rows, :]
        OUT[rows, :] = mid + PV[7:8, :]
        unit, _ = unit_of(mid)
        h2 = (unit * PV[5:6, :] + PV[6:7, :]).astype(BF)
        N2[rows, :] = h2
        HT[:, rows] = h2.T
        return carry

    loop("second_norm", 0, NSEQ, out_step, 0)
    o_wait(2)
    for p in (10, 11, 12):
        c_wait(p)

    chunks = [(i % NS, i, 0, D) for i in range(8)] + [(8 % NS, 8, 0, 384), (8 % NS, 8, 384, 384)]
    gcopies = {}

    @partial(scoped, "acquire")
    def acquire(i):
        if i >= NS:
            for cp in gcopies.pop(i - NS):
                settle(cp)

    @partial(scoped, "step0")
    def step0(i):
        slot, at, r0, rows = chunks[i]
        if NS <= i <= 8 and comm:
            pl.semaphore_wait(credit, 1)
        rr = pl.ds(r0, rows)
        gcopies[i] = [
            send(
                G.at[slot, 2 * t + 1 - c, rr],
                RC.at[slot, t, rr],
                cs.at[i, t],
                cr.at[i, t],
                core,
            )
            for t in range(2)
        ]

    def addto(dst, one, two, rows, strip=64):
        def step(r, carry):
            sl = ds(r * strip, strip)
            dst[sl, :] = (one[sl, :].astype(F32) + two[sl, :].astype(F32)).astype(BF)
            return carry

        lax.fori_loop(0, rows // strip, step, 0)

    @partial(scoped, "step1")
    def step1(i):
        slot, at, r0, rows = chunks[i]
        rr = pl.ds(r0, rows)
        got(RC.at[slot, 0, rr], cs.at[i, 0], cr.at[i, 0], core)
        got(RC.at[slot, 1, rr], cs.at[i, 1], cr.at[i, 1], core)
        gs = G.at[slot, ny, rr]
        addto(gs, gs, RC.at[slot, 1 - yy, rr], rows)
        gcopies[i].append(send(gs, RY.at[at, rr], ys.at[i], yr.at[i], ypart))
        addto(A.at[at, rr], G.at[slot, n, rr], RC.at[slot, yy, rr], rows)
        if i + NS <= 8 and comm:
            pl.semaphore_signal(credit, inc=1, device_id=core, device_id_type=MESH)

    def halves(i):
        slot, at, r0, rows = chunks[i]
        half = rows // 2
        return at, r0, half, ds(r0 + b * half, half, 16), ds(r0 + (1 - b) * half, half, 16)

    @partial(scoped, "step2")
    def step2(i):
        at, r0, half, mine, other = halves(i)
        got(RY.at[at, pl.ds(r0, 2 * half)], ys.at[i], yr.at[i], ypart)
        addto(A.at[at, other], A.at[at, other], RY.at[at, other], half)
        rx = RX.at[at, pl.ds(r0 // 2, half)]
        send(A.at[at, other], rx, xs.at[i], xr.at[i], xpart)
        addto(A.at[at, mine], A.at[at, mine], RY.at[at, mine], half)

    def quarter(i, part):
        at, r0, half, mine, other = halves(i)
        q = half // 4
        return ds(r0 + b * half + part * q, q, 16), pl.ds(r0 // 8, q)

    @partial(scoped, "step3")
    def step3(i):
        at, r0, half, mine, other = halves(i)
        rx = RX.at[at, pl.ds(r0 // 2, half)]
        got(rx, xs.at[i], xr.at[i], xpart)
        addto(A.at[at, mine], A.at[at, mine], rx, half)
        for k in (2, 1, 3):
            there, here = quarter(i, zt[k])
            send(
                A.at[at, there],
                RZ.at[at, k - 1, here],
                zs.at[i, k - 1],
                zr.at[i, k - 1],
                zpart[k],
            )

    def place(i, half, part):
        slot, at, r0, rows = chunks[i]
        size = rows // 8
        return RY.at[at, ds(r0 + (half * 4 + part) * size, size, 16)]

    locals_ = []

    @partial(scoped, "step4")
    def step4(i):
        slot, at, r0, rows = chunks[i]
        there, here = quarter(i, z)
        for k in range(1, 4):
            got(RZ.at[at, k - 1, here], zs.at[i, k - 1], zr.at[i, k - 1], zpart[k])
        t = A[at, there, :].astype(F32)
        for k in range(3):
            t = t + RZ[at, k, here, :].astype(F32)
        dst = place(i, b, z)
        if not extra:
            dst[...] = t.astype(BF)
        else:
            last = A.at[at, there]
            last[...] = t.astype(BF)
            for e in range(extra):
                one, two = RE.at[at, e, here], RZ.at[at, e, here]
                send(last, one, es.at[i, e], er.at[i, e], epart[e])
                got(one, es.at[i, e], er.at[i, e], epart[e])
                two[...] = (last[...].astype(F32) + one[...].astype(F32)).astype(BF)
                last = two
            dst[...] = last[...]
        for k in (2, 1, 3):
            send(dst, dst, zgs.at[i, k - 1], zgr.at[i, k - 1], zpart[k])
        send(dst, dst, xgs.at[i, 0], xgr.at[i, 0], xpart)

    @partial(scoped, "step5")
    def step5(i):
        for k in (1, 3, 2):
            dst = place(i, b, zf[k])
            got(dst, zgs.at[i, k - 1], zgr.at[i, k - 1], zpart[k])
            send(dst, dst, xgs.at[i, k], xgr.at[i, k], xpart)

    @partial(scoped, "step6")
    def step6(i):
        slot, at, r0, rows = chunks[i]
        for k in (0, 1, 3, 2):
            got(place(i, 1 - b, zf[k]), xgs.at[i, k], xgr.at[i, k], xpart)
        rr = pl.ds(r0, rows)
        cp = pltpu.make_async_copy(RY.at[at, rr], g_out.at[at, rr], fsem.at[i])
        cp.start()
        locals_.append(cp)

    steps = (step0, step1, step2, step3, step4, step5, step6)

    def run(*todo):
        for k, i in todo:
            steps[k](i)

    def wait_w2(j):
        o_wait(3 + j)
        c_wait(13 + j)

    after = {
        (0, 0): ((y_pass, 14), (x_pass, 13)),
        (0, 1): ((step0, 0), (wait_w2, 0)),
        (0, 2): ((step1, 0), (y_pass, 15), (x_pass, 14)),
        (0, 3): ((step0, 1),),
        (0, 4): ((step1, 1), (wait_w2, 1)),
        (0, 5): ((x_pass, 15),),
        (1, 0): ((wait_w2, 2), (step2, 0)),
        (1, 1): ((step0, 2),),
        (1, 2): ((step1, 2),),
        (1, 3): ((step0, 3), (step3, 0), (step2, 1)),
        (1, 4): ((step1, 3),),
        (1, 5): ((step4, 0),),
        (2, 0): ((step3, 1),),
        (2, 1): ((step0, 4), (step2, 2)),
        (2, 2): ((step1, 4), (step5, 0), (step4, 1)),
        (2, 3): ((step0, 5), (step3, 2)),
        (2, 4): ((step1, 5),),
        (2, 5): ((step2, 3), (step6, 0), (step5, 1)),
    }

    def service(*key):
        for fn, i in after[key]:
            fn(i)

    for j in range(3):
        s2, s1 = (2 * j) % NS, (2 * j + 1) % NS

        def hidden(s, carry, j=j):
            col = ds(s * 768 + j * 256, 256)
            sc = ds(s * 256, 256)
            act, slope = gelu_pair(mm(N2[...], W1[:, col]) + B1[:, col])
            ACT[:, sc] = act.astype(BF)
            DPR[:, sc] = slope.astype(BF)
            return carry

        loop("hidden", 0, 4, hidden, 0)
        service(j, 0)
        acquire(2 * j)

        def fc2_grad(s, carry):
            G[s2, s] = mm(GT[...], ACT[:, ds(s * 256, 256)]).astype(BF)
            return carry

        loop("fc2_grad", 0, 4, fc2_grad, 0)
        service(j, 1)

        def hidden_back(s, carry, j=j):
            sc = ds(s * 256, 256)
            dpre = mm_nt(CB[...], W2[j, sc, :]) * DPR[:, sc].astype(F32)
            DPR[:, sc] = dpre.astype(BF)
            V[ds(8 + s, 1, 1), pl.ds(j * 256, 256)] = colsum(dpre)
            return carry

        loop("hidden_back", 0, 4, hidden_back, 0)
        if j == 2:
            cot2 = pltpu.make_async_copy(cot, CB, lsem.at[1])
            cot2.start()
        service(j, 2)
        acquire(2 * j + 1)

        def fc1_grad(s, carry):
            res = mm(HT[...], DPR[:, ds(s * 256, 256)]).astype(BF)
            for m in range(4):
                G[s1, m, ds(s * 192, 192), :] = res[192 * m : 192 * m + 192, :]
            return carry

        loop("fc1_grad", 0, 4, fc1_grad, 0)
        service(j, 3)

        def accum_out(i, carry, j=j):
            col = ds(i * 256, 256)
            OUT[:, col] += mm(ACT[...], W2[j, :, col])
            return carry

        if j < 2:
            loop("accum_out", 0, 3, accum_out, 0)
        service(j, 4)

        def accum_back(i, carry, j=j):
            col = ds(i * 256, 256)
            t = mm_nt(DPR[:, pl.ds(0, 256)], W1[col, pl.ds(j * 256, 256)])
            for s in range(1, 4):
                t = t + mm_nt(
                    DPR[:, pl.ds(s * 256, 256)], W1[col, pl.ds(s * 768 + j * 256, 256)]
                )
            DH[:, col] = t if j == 0 else DH[:, col] + t
            return carry

        loop("accum_back", 0, 3, accum_back, 0)
        service(j, 5)

    cot2.wait()

    def ln2_step(r, carry):
        sg, sb, so = carry
        rows = ds(r * L, L)
        dh = DH[rows, :]
        unit, inv = unit_of(MID[rows, :])
        g2 = CB[rows, :].astype(F32) * SW[r][0:1, 0:1] + norm_back(dh, unit, inv, PV[5:6, :])
        DH[rows, :] = g2
        g2b = g2.astype(BF)
        N2[rows, :] = g2b
        unit1, _ = unit_of(PT[rows, :].astype(F32))
        GT[:, rows] = (unit1 * PV[0:1, :] + PV[1:2, :]).astype(BF).T
        return sg + colsum(dh * unit), sb + colsum(dh), so + colsum(g2)

    zero = jnp.zeros((1, D), F32)
    sums = loop("second_norm_back", 0, 2, ln2_step, (zero, zero, zero))
    run((4, 2))
    sums = loop("second_norm_back", 2, 4, ln2_step, sums)
    V[5:6, :], V[6:7, :], V[4:5, :] = sums
    run((3, 3))

    def put_block(blk, res):
        slot, cb = lax.rem(6 + lax.div(blk, 4), NS), lax.rem(blk, 4)
        for m in range(4):
            G[slot, m, ds(cb * 192, 192), :] = res[192 * m : 192 * m + 192, :]

    acquire(6)

    def out_grad(i, carry):
        put_block(i, mm(AT[...], N2[:, ds(256 * i, 256)]).astype(BF))
        return carry

    loop("out_grad", 0, 3, out_grad, 0)

    def att_grad(i, carry):
        col = ds(i * 256, 256)
        CB[:, col] = mm_nt(N2[...], Wo[col, :]).astype(BF)
        return carry

    loop("att_grad", 0, 3, att_grad, 0)
    run((2, 4))

    def attend_back(seq, hq):
        drop = drops(seq)

        def one(hp):
            rows = ds(seq * L, L)
            cq, ck, cv = ds(hp * 128, 128), ds(D + hp * 128, 128), ds(2 * D + hp * 128, 128)
            q = QKV[rows, cq] * BF(SCALE)
            k = QKV[rows, ck]
            v = QKV[rows, cv]
            do = CB[rows, cq]
            kt = k.T
            dq, dk, dv = [], [], []
            for h in range(2):
                s = scores(q, k, drop, h)
                p = jnp.exp(s - LSE[ds(seq * 2 * HP + hp * 2 + h, 1, 1), :])
                dp = mm_nt(v, do * masks[h])
                dsc = (p * (dp - colsum(dp * p))).astype(BF)
                dv.append(mm(p.astype(BF), do))
                dk.append(mm(dsc, q))
                dq.append(mm(kt[64 * h : 64 * h + 64, :], dsc))
            dqt = (jnp.concatenate(dq, axis=0) * SCALE).astype(BF)
            QKV[rows, cq] = dqt.T
            QKV[rows, ck] = jnp.where(lowf, dk[0], dk[1]).astype(BF)
            QKV[rows, cv] = jnp.where(lowf, dv[0], dv[1]).astype(BF)

        for t in range(2):
            one(2 * hq + t)

    between = {
        (0, 0): ((step5, 2), (step6, 1)),
        (0, 1): ((step4, 3), (step3, 4)),
        (0, 2): ((step0, 6), (step2, 5)),
        (1, 0): ((step1, 6), (step6, 2), (step5, 3)),
        (1, 1): ((step4, 4), (step3, 5)),
        (1, 2): ((step0, 7),),
        (2, 0): ((step1, 7), (step5, 4), (step2, 6)),
        (2, 1): ((step4, 5), (step6, 3)),
        (2, 2): ((step1, 8), (step0, 9), (step1, 9)),
    }

    def serve(*key):
        for fn, i in between[key]:
            fn(i)

    for hq in range(3):

        def seq_step(seq, carry, hq=hq):
            attend_back(seq, hq)
            return carry

        loop("attend_back", 0, 2, seq_step, 0)
        serve(hq, 0)
        loop("attend_back", 2, 4, seq_step, 0)
        serve(hq, 1)
        if hq < 2:
            acquire(7 + hq)

        def qkv_grad(t, carry, hq=hq):
            put_block(3 + 3 * hq + t, mm(GT[...], QKV[:, ds(t * D + hq * 256, 256)]).astype(BF))
            return carry

        loop("qkv_grad", 0, 1, qkv_grad, 0)
        if hq == 2:
            step0(8)
        loop("qkv_grad", 1, 3, qkv_grad, 0)
        serve(hq, 2)
        V[2:3, pl.ds(hq * 256, 256)] = colsum(QKV[:, pl.ds(hq * 256, 256)].astype(F32))
        V[3:4, pl.ds(hq * 256, 256)] = colsum(QKV[:, pl.ds(2 * D + hq * 256, 256)].astype(F32))

    def out_last(i, carry):
        col = ds(i * 256, 256)
        N1[:, col] = (OUT[:, col] + mm(ACT[...], W2[2, :, col])).astype(BF)
        return carry

    def input_block(i, carry):
        col = ds(i * 256, 256)
        OUT[:, col] = mm_nt(QKV[...], Wq[col, :])
        return carry

    def ln1_back(r, carry):
        sg, sb = carry
        rows = ds(r * L, L)
        dh = OUT[rows, :]
        unit, inv = unit_of(PT[rows, :].astype(F32))
        MID[rows, :] = DH[rows, :] + norm_back(dh, unit, inv, PV[0:1, :])
        return sg + colsum(dh * unit), sb + colsum(dh)

    run((3, 6))
    loop("out_last", 0, 3, out_last, 0)
    bo_cp = pltpu.make_async_copy(N1, bo_out, lsem.at[9])
    bo_cp.start()
    run((5, 5), (2, 7))
    loop("input_grad", 0, 2, input_block, 0)
    run((4, 6), (2, 8))
    loop("input_grad", 2, 3, input_block, 0)
    run((6, 4), (3, 7))
    carry = loop("first_norm_back", 0, NSEQ, ln1_back, (zero, zero))
    V[0:1, :] = carry[0]
    V[1:2, :] = carry[1]
    pg_cp = pltpu.make_async_copy(MID, pg_out, lsem.at[10])
    pg_cp.start()

    send(V, VR.at[0], vs.at[0], vr.at[0], core)
    run((2, 9), (3, 8))
    got(VR.at[0], vs.at[0], vr.at[0], core)
    VB[0] = V[...] + VR[0]
    send(VB.at[0], VR.at[1], vs.at[1], vr.at[1], ypart)
    run((5, 6), (4, 7), (3, 9))
    got(VR.at[1], vs.at[1], vr.at[1], ypart)
    VB[1] = VB[0] + VR[1]
    send(VB.at[1], VR.at[2], vs.at[2], vr.at[2], xpart)
    run((4, 8), (6, 5))
    got(VR.at[2], vs.at[2], vr.at[2], xpart)
    VB[2] = VB[1] + VR[2]
    PB[z] = VB[2]
    for k in range(1, 4):
        send(VB.at[2], PB.at[z], vs.at[2 + k], vr.at[2 + k], zpart[k])
    run((4, 9), (5, 7), (5, 8))
    for k in range(1, 4):
        got(PB.at[zf[k]], vs.at[2 + k], vr.at[2 + k], zpart[k])
    tot = PB[0] + PB[1] + PB[2] + PB[3]
    for e in range(extra):
        VE[2 * e] = tot
        send(VE.at[2 * e], VE.at[2 * e + 1], vs.at[6 + e], vr.at[6 + e], epart[e])
        got(VE.at[2 * e + 1], vs.at[6 + e], vr.at[6 + e], epart[e])
        tot = tot + VE[2 * e + 1]
    v_out[...] = tot
    run((5, 9), (6, 6), (6, 7))
    for i in (8, 9):
        step6(i)
    for cp in list(sent):
        cp.wait_send()
    if comm:
        gather_done()
    for cp in locals_:
        cp.wait()
    bo_cp.wait()
    pg_cp.wait()


def layer_call(extra, args, comm=True):
    any_, vmem, smem = (
        pl.BlockSpec(memory_space=s) for s in (pl.ANY, pltpu.VMEM, pltpu.SMEM)
    )
    dma, reg = pltpu.SemaphoreType.DMA, pltpu.SemaphoreType.REGULAR
    ex = max(extra, 1)
    scratch = [
        pltpu.VMEM((D, QW), BF),
        pltpu.VMEM((D, D), BF),
        pltpu.VMEM((D, FF), BF),
        pltpu.VMEM((3, 1024, D), BF),
        pltpu.VMEM((TOK, QW), BF),
        pltpu.VMEM((TOK, D), BF),
        pltpu.VMEM((TOK, D), BF),
        pltpu.VMEM((D, TOK), BF),
        pltpu.VMEM((D, TOK), BF),
        pltpu.VMEM((D, TOK), BF),
        pltpu.VMEM((TOK, D), BF),
        pltpu.VMEM((TOK, D), BF),
        pltpu.VMEM((TOK, D), F32),
        pltpu.VMEM((TOK, D), F32),
        pltpu.VMEM((TOK, D), F32),
        pltpu.VMEM((TOK, 1024), BF),
        pltpu.VMEM((TOK, 1024), BF),
        pltpu.VMEM((NSEQ * 2 * HP, L), F32),
        pltpu.VMEM((4, 16, D), F32),
        pltpu.VMEM((16, D), F32),
        pltpu.VMEM((16, D), F32),
        pltpu.VMEM((1, FF), F32),
        pltpu.VMEM((1, QW), F32),
        pltpu.VMEM((NSEQ, 8, 128), F32),
        pltpu.VMEM((16, D), F32),
        pltpu.VMEM((3, 16, D), F32),
        pltpu.VMEM((3, 16, D), F32),
        pltpu.VMEM((2 * ex, 16, D), F32),
        pltpu.VMEM((NS, 4, D, 256), BF),
        pltpu.VMEM((NS, 2, D, 256), BF),
        pltpu.VMEM((CH, D, 256), BF),
        pltpu.VMEM((CH, D, 256), BF),
        pltpu.VMEM((CH, 384, 256), BF),
        pltpu.VMEM((CH, 3, 96, 256), BF),
        pltpu.VMEM((CH if extra else 1, ex, 96 if extra else 16, 256), BF),
        dma((11,)),
        dma((NC,)),
        dma((2, 3)),
        dma((8,)),
        dma((8,)),
    ]
    scratch += [dma((NP,))] * 8
    scratch += [dma((NC, 2)), dma((NC, 2)), reg]
    scratch += [dma((NC,))] * 4
    scratch += [dma((NC, 3))] * 2
    scratch += [dma((NC, ex))] * 2
    scratch += [dma((NC, 3))] * 2
    scratch += [dma((NC, 4))] * 2
    scratch += [dma((6 + ex,))] * 2
    out_shape = (
        jax.ShapeDtypeStruct((TOK, D), BF),
        jax.ShapeDtypeStruct((TOK, D), F32),
        jax.ShapeDtypeStruct((CH, D, 256), BF),
        jax.ShapeDtypeStruct((16, D), F32),
    )
    return pl.pallas_call(
        partial(kernel, extra, comm),
        out_shape=out_shape,
        in_specs=[smem] + [vmem] * 10 + [any_] * 6,
        out_specs=[any_] * 3 + [vmem],
        scratch_shapes=scratch,
        compiler_params=pltpu.CompilerParams(
            collective_id=0 if comm else None, has_side_effects=True, vmem_limit_bytes=67_030_000
        ),
        name="layer",
    )(*args)


def body(
    comm,
    extra,
    patches,
    key_lengths,
    tile_counts,
    ln1_gain,
    ln1_bias,
    qkv_weight,
    query_bias,
    value_bias,
    out_weight,
    out_bias,
    ln2_gain,
    ln2_bias,
    fc1_weight,
    fc1_bias,
    fc2_weight,
    fc2_bias,
    out_cot,
):
    bo, pg, grads, vec = layer_call(
        extra,
        (
            key_lengths,
            tile_counts.reshape(1, -1),
            ln1_gain,
            ln1_bias,
            query_bias,
            value_bias,
            out_bias,
            ln2_gain,
            ln2_bias,
            fc2_bias,
            fc1_bias,
            patches.reshape(TOK, D),
            out_cot.reshape(TOK, D),
            qkv_weight,
            out_weight,
            fc1_weight,
            fc2_weight,
        ),
        comm,
    )
    return finish_call(bo, pg, grads, vec)


def finish(
    vec_in,
    bo,
    pg,
    grads,
    bo_out,
    pg_out,
    l1g,
    l1b,
    qkv_out,
    qb,
    vb,
    out_out,
    ob,
    l2g,
    l2b,
    fc1_out,
    f1b,
    fc2_out,
    f2b,
    GB,
    PGV,
    BOV,
    vec,
    FQ,
    FO,
    F1,
    F2,
    isem,
    csem,
    osem,
):
    n = lax.axis_index("narrow")
    loads = [pltpu.make_async_copy(grads.at[i], GB.at[i], isem.at[i]) for i in range(CH)]
    vec_cp = pltpu.make_async_copy(vec_in, vec, csem.at[8])
    vec_cp.start()
    for cp in loads[:3]:
        cp.start()
    for cp in loads[3:]:
        cp.start()
    through = []
    for q in range(NSEQ):
        through.append((pg.at[q], PGV.at[q], pg_out.at[q]))
        through.append((bo.at[q], BOV.at[q], bo_out.at[q]))
    stops = [pltpu.make_async_copy(a, h, csem.at[k]) for k, (a, h, _) in enumerate(through)]
    for cp in stops:
        cp.start()
    done = []

    def leave(src, dst):
        cp = pltpu.make_async_copy(src, dst, osem.at[len(done)])
        cp.start()
        done.append(cp)

    for i in range(CH):
        loads[i].wait()
        if i < 6 and i % 2 == 0:
            rows = pl.ds((i // 2) * 256, 256)
            F2[rows, :] = GB[i].T.astype(F32)
            leave(F2.at[rows], fc2_out.at[rows])
            continue
        for k in range(4):
            piece = GB[i, pl.ds(192 * k, 192), :].astype(F32)
            if i < 6:
                held, out, col = F1, fc1_out, k * 768 + (i // 2) * 256
            else:
                blk = 4 * (i - 6) + k
                held, out, col = FO, out_out, blk * 256
                if blk >= 3:
                    held, out, col = FQ, qkv_out, ((blk - 3) % 3) * D + ((blk - 3) // 3) * 256
            held[:, pl.ds(col, 256)] = piece
            leave(held.at[:, pl.ds(col, 256)], out.at[:, pl.ds(col, 256)])
    for cp, (_, held, out) in zip(stops, through):
        cp.wait()
        leave(held, out)
    vec_cp.wait()
    for m in range(4):

        @pl.when(n == m)
        def _():
            for r, one in enumerate((l1g, l1b, qb, vb, ob, l2g, l2b, f2b)):
                one[...] = vec[r, 192 * m : 192 * m + 192]
            f1b[...] = vec[8 + m, :]

    for cp in done:
        cp.wait()


def finish_call(bo, pg, grads, vec):
    vmem, hbm = (pl.BlockSpec(memory_space=s) for s in (pltpu.VMEM, pltpu.HBM))
    small = jax.ShapeDtypeStruct((192,), F32)
    shapes = [
        jax.ShapeDtypeStruct((NSEQ, L, D), BF),
        jax.ShapeDtypeStruct((NSEQ, L, D), F32),
        small,
        small,
        jax.ShapeDtypeStruct((192, QW), F32),
        small,
        small,
        jax.ShapeDtypeStruct((192, D), F32),
        small,
        small,
        small,
        jax.ShapeDtypeStruct((192, FF), F32),
        jax.ShapeDtypeStruct((D,), F32),
        jax.ShapeDtypeStruct((D, D), F32),
        small,
    ]
    dma = pltpu.SemaphoreType.DMA
    return pl.pallas_call(
        finish,
        out_shape=shapes,
        in_specs=[hbm] * 4,
        out_specs=[hbm if len(s.shape) > 1 else vmem for s in shapes],
        scratch_shapes=[
            pltpu.VMEM((CH, D, 256), BF),
            pltpu.VMEM((NSEQ, L, D), F32),
            pltpu.VMEM((NSEQ, L, D), BF),
            pltpu.VMEM((16, D), F32),
            pltpu.VMEM((192, QW), F32),
            pltpu.VMEM((192, D), F32),
            pltpu.VMEM((192, FF), F32),
            pltpu.VMEM((D, D), F32),
            dma((CH,)),
            dma((9,)),
            dma((40,)),
        ],
        compiler_params=pltpu.CompilerParams(vmem_limit_bytes=64 * 1000 * 1000),
        name="finish",
    )(vec, bo.reshape(NSEQ, L, D), pg.reshape(NSEQ, L, D), grads)


def solution(mesh, comm=True):
    extra = (mesh.shape["wide"] // 8).bit_length() - 1
    rows3 = P(("wide", "narrow"), None, None)
    mat, vec = P("narrow", None), P("narrow")
    in_specs = (
        rows3,
        P(("wide", "narrow")),
        P(),
        vec,
        vec,
        mat,
        vec,
        vec,
        mat,
        vec,
        vec,
        vec,
        mat,
        vec,
        mat,
        vec,
        rows3,
    )
    out_specs = (
        rows3,
        rows3,
        vec,
        vec,
        mat,
        vec,
        vec,
        mat,
        vec,
        vec,
        vec,
        mat,
        vec,
        mat,
        vec,
    )
    return jax.shard_map(
        partial(body, comm, extra), mesh=mesh, in_specs=in_specs, out_specs=out_specs, check_vma=False
    )
```
